32 devices in a mesh: parts: 2 (over y), shard: 4 (over z), grp: 2 (over x), rep: 2 (over core).
Axes of the slice: x: 2, y: 2, z: 4, core: 2. Of those that a mesh axis runs over, the one named last changes fastest.
Arguments:
- embeddings: float32 [4096, 768], P(('parts', 'shard', 'grp', 'rep')), parts along dimension 0, may hold values from -6 to 6
- clusters: int32 [4096, 1], P(('parts', 'shard', 'grp', 'rep')), parts along dimension 0, may hold values from 0 to 7; in each aligned block of 128 rows (0 to 127, 128 to 255, ...) at most 32 rows name the same one
Outputs:
- dup_weight: float32 [4096], P(('parts', 'shard', 'grp', 'rep')), parts along dimension 0
The draws below stay inside these ranges and needn't reach their ends.
There are 2 independent parts, one for each index of `parts`. The reference program is written for one: setup_inputs(seed, part) draws one part's arguments, and reference() takes and returns one part's arrays. A program takes and returns all parts, laid end to end along the dimension named above; each array names one. Nothing has to cross between parts.
Inputs may be any that keep to these rules, and one draw needn't show every extreme that they name: `clusters`: among the rows of one device, at most 32 belong to any one cluster, and some cluster has exactly 32 of them.
All inputs are finite; a program needn't handle non-finite values.
Results may differ from the reference program's by a relative error of at most 0.00035.
Values may be sent and summed in bfloat16 or wider, within the bound.
A program may use at most 64 MiB of HBM per device.

```python
import math
import jax
import jax.numpy as jnp
import numpy as np
from jax import lax

D = 768
ROW_DEV = 128
CLUSTERS = 8
CAP = 32
ROWS = 2048
N_SHARD = 4
N_GRP = 2
N_REP = 2


def block_scale(stream_key, dims, pieces, least, largest):
    gain = 1.0
    for dim, blocks in pieces:
        heights = jax.random.uniform(jax.random.fold_in(jax.random.fold_in(stream_key, 6), dim), (blocks,), jnp.float32, least / len(pieces), largest / len(pieces))
        gain = gain * jnp.repeat(jnp.exp(heights), dims[dim] // blocks).reshape((-1,) + (1,) * (len(dims) - 1 - dim))
    return gain


def deal_out(rng, own, number, rows, number_of, top, most, slope):
    order = jax.random.permutation(rng, number_of)
    crowded, ordinary = shares(number_of, rows * top, most, slope, True), shares(number_of, rows * top, most, slope, False)
    places = jnp.arange(number_of)

    def named(lengths, turn):
        used = int((lengths > 0).sum())
        fixed = max(1, used // 4)
        passed = fixed + (places - fixed + turn * (used - fixed)) % max(1, number_of - fixed)
        return jnp.zeros((number_of,), jnp.int32).at[order[jnp.where(places < fixed, places, passed)]].set(jnp.asarray(lengths, jnp.int32))

    lengths = jnp.where(number % 4 == 0, named(crowded, number // 4), named(ordinary, number - number // 4 - 1))
    mixed = jax.random.permutation(jax.random.fold_in(own, 3), number_of)
    source_of, receiver = mixed[0:number_of // 2 * 2:2], mixed[1:number_of // 2 * 2:2]
    room = jnp.minimum(lengths[source_of] - 1, most - lengths[receiver]) // 2
    room = jnp.where((source_of == order[0]) | (receiver == order[0]) | (lengths[receiver] == 0), 0, jnp.maximum(room, 0))
    passed = jax.random.randint(jax.random.fold_in(own, 4), (number_of // 2,), 0, 1 << 20) % (room + 1)
    lengths = lengths.at[source_of].add(-passed).at[receiver].add(passed)
    items = jnp.searchsorted(jnp.cumsum(lengths), jnp.arange(rows * top), side="right").astype(jnp.int32)
    listing = items.reshape(top, rows).T
    listing = listing[jax.random.permutation(jax.random.fold_in(own, 1), rows)]
    turn = jax.random.randint(jax.random.fold_in(own, 2), (rows, 1), 0, top)
    return jnp.take_along_axis(listing, (jnp.arange(top)[None, :] + turn) % top, axis=1)


def shares(number_of, total, reach, slope, full):
    loads = [(1 << 20) // math.isqrt(standing ** slope) + 1 for standing in range(1, number_of + 1)]
    largest = reach if full else min(reach, max(-(-total // number_of), total * loads[0] // sum(loads)))
    least = 1 if total - largest >= number_of - 1 else 0
    holding, surplus = [largest] + [least] * (number_of - 1), total - largest - least * (number_of - 1)
    while surplus > 0:
        free = [i for i in range(1, number_of) if holding[i] < largest] or [i for i in range(1, number_of) if holding[i] < reach]
        pool, left = sum([loads[i] for i in free]), surplus
        for i in free:
            addition = min(reach - holding[i], max(1, left * loads[i] // pool), surplus)
            holding[i] = holding[i] + addition
            surplus = surplus - addition
    return np.array(holding)


def centred(stream_key, shape, scale, bound, cuts=(), held_as=jnp.bfloat16):
    array = scale * jax.random.normal(stream_key, shape, jnp.float32)
    if cuts:
        array = array * block_scale(stream_key, shape, cuts, -0.22, 0.18)
    return jnp.clip(array, -bound, bound).astype(held_as)


def setup_inputs(seed: int = 0, part: int = 0) -> dict:
    key_of = jax.random.split(jax.random.key(seed), 3)
    part_keys = jax.random.split(jax.random.fold_in(key_of[2], part), 3)
    embeddings = centred(part_keys[0], (ROWS, D), 1.0, 6.0, ((0, 16),), jnp.float32)
    clusters_keys = jax.random.split(jax.random.fold_in(part_keys[1], 1), ROWS // ROW_DEV)
    clusters_turns = jax.random.permutation(jax.random.fold_in(part_keys[1], 3), ROWS // ROW_DEV)
    clusters = jax.vmap(lambda own, number: deal_out(jax.random.fold_in(part_keys[1], 2), own, number, ROW_DEV, CLUSTERS, 1, CAP, 2))(clusters_keys, clusters_turns).reshape((ROWS, 1))
    return dict(embeddings=embeddings, clusters=clusters)


sharpness = 60.0

def unit_rows(matrix):
    inverse = lax.rsqrt(lax.optimization_barrier(jnp.sum(matrix * matrix, axis=1, keepdims=True)) + 1e-06)
    return (matrix * inverse).astype(jnp.bfloat16)

def reference(embeddings, clusters):
    normed = unit_rows(embeddings)
    cluster_of = clusters[:, 0].astype(jnp.int32)
    row_count = cluster_of.shape[0]
    feature_dim = normed.shape[1]
    sort_order = jnp.argsort(cluster_of, stable=True).astype(jnp.int32)
    sorted_unit = normed[sort_order]
    sorted_ids = cluster_of[sort_order]
    max_members = N_SHARD * N_GRP * N_REP * CAP
    block_rows = 512 if row_count % 512 == 0 else row_count
    padded_unit = jnp.concatenate([jnp.zeros((max_members, feature_dim), normed.dtype), sorted_unit, jnp.zeros((max_members, feature_dim), normed.dtype)], axis=0)
    padded_ids = jnp.concatenate([jnp.full((max_members,), -1, jnp.int32), sorted_ids, jnp.full((max_members,), -1, jnp.int32)], axis=0)

    def block_sums(block_index):
        first_row = (block_index * block_rows).astype(jnp.int32)
        queries = lax.dynamic_slice_in_dim(sorted_unit, first_row, block_rows, 0)
        query_ids = lax.dynamic_slice_in_dim(sorted_ids, first_row, block_rows, 0)
        key_rows = lax.dynamic_slice_in_dim(padded_unit, first_row, block_rows + 2 * max_members, 0)
        key_ids = lax.dynamic_slice_in_dim(padded_ids, first_row, block_rows + 2 * max_members, 0)
        scores = lax.dot_general(queries, key_rows, (((1,), (1,)), ((), ())), preferred_element_type=jnp.float32)
        query_pos = first_row + jnp.arange(block_rows, dtype=jnp.int32)
        key_pos = first_row - max_members + jnp.arange(block_rows + 2 * max_members, dtype=jnp.int32)
        paired = (query_ids[:, None] == key_ids[None, :]) & (query_pos[:, None] != key_pos[None, :])
        return lax.optimization_barrier(jnp.sum(jnp.where(paired, jnp.exp(sharpness * scores), 0.0), axis=1))
    partial_mass = lax.map(block_sums, jnp.arange(row_count // block_rows, dtype=jnp.int32)).reshape(row_count)
    mass = jnp.zeros((row_count,), partial_mass.dtype).at[sort_order].set(partial_mass)
    return jnp.log1p(mass)
```

```python
import functools

import jax
import jax.numpy as jnp
from jax import lax
from jax.experimental import pallas as pl
from jax.experimental.pallas import tpu as pltpu
from jax.sharding import PartitionSpec as P

sharpness = 60.0


def from_partner(value, axis, distance):
    mask = 2**distance
    pairs = [(source, source ^ mask) for source in range(lax.axis_size(axis))]
    return lax.ppermute(value, axis, pairs)


def unit_rows(matrix):
    inverse = lax.rsqrt(jnp.sum(matrix * matrix, axis=1, keepdims=True) + 1e-06)
    return (matrix * inverse).astype(jnp.bfloat16)


def collective_body(embeddings, clusters):
    shard_count = lax.axis_size("shard")
    group_count = lax.axis_size("grp")
    owners = shard_count * group_count
    row_count = embeddings.shape[0]
    feature_dim = embeddings.shape[1]
    capacity = 2 * row_count // owners
    normed = unit_rows(embeddings)
    cluster_of = clusters[:, 0]
    member_table = (cluster_of[:, None] == jnp.arange(owners, dtype=jnp.int32)[None, :]).astype(
        jnp.float32
    )
    earlier = (jnp.arange(row_count)[:, None] > jnp.arange(row_count)[None, :]).astype(jnp.float32)
    preceding = jnp.dot(
        earlier, member_table, precision=lax.Precision.HIGHEST, preferred_element_type=jnp.float32
    )
    position = jnp.sum(preceding * member_table, axis=1).astype(jnp.int32)
    slot_index = cluster_of * capacity + position
    outgoing = jnp.zeros((owners * capacity, feature_dim), jnp.bfloat16).at[slot_index].set(normed)
    present = jnp.zeros((owners * capacity,), jnp.int32).at[slot_index].set(1)
    arrived, arrived_live = (
        lax.all_to_all(
            outgoing.reshape(owners, capacity, feature_dim),
            ("shard", "grp"),
            split_axis=0,
            concat_axis=0,
            tiled=True,
        ),
        lax.all_to_all(
            present.reshape(owners, capacity),
            ("shard", "grp"),
            split_axis=0,
            concat_axis=0,
            tiled=True,
        ),
    )
    slot_count = owners * capacity
    local_rows = arrived.reshape(slot_count, feature_dim)
    local_live = arrived_live.reshape(slot_count)
    partner, partner_live = from_partner((local_rows, local_live), "rep", 0)
    key_rows = jnp.concatenate([local_rows, partner], axis=0)
    key_live = jnp.concatenate([local_live, partner_live], axis=0) > 0
    key_pos = jnp.arange(2 * slot_count, dtype=jnp.int32)

    def block_sums(block_index):
        first_row = block_index * slot_count
        scores = lax.dot_general(
            local_rows, key_rows, (((1,), (1,)), ((), ())), preferred_element_type=jnp.float32
        )
        query_pos = first_row + jnp.arange(slot_count, dtype=jnp.int32)
        paired = key_live[None, :] & (query_pos[:, None] != key_pos[None, :])
        return jnp.sum(jnp.where(paired, jnp.exp(sharpness * scores), 0.0), axis=1)

    partial_mass = lax.map(
        block_sums, jnp.arange(slot_count // slot_count, dtype=jnp.int32)
    ).reshape(slot_count)
    returned = lax.all_to_all(
        partial_mass.reshape(owners, capacity),
        ("shard", "grp"),
        split_axis=0,
        concat_axis=0,
        tiled=True,
    )
    mass = returned.reshape(slot_count)[slot_index]
    return jnp.log1p(mass)


def ring_distance(step, size):
    return min(step, size - step)


def kernel(sizes, capacity, rows_hbm, cluster_ref, mass_ref, rows, outgoing, gathered, mass, returned,
           load_sem, send_sem, recv_sem, reply_send_sem, reply_recv_sem):
    n_shard, n_grp, n_rep = sizes
    shard, grp, rep = lax.axis_index("shard"), lax.axis_index("grp"), lax.axis_index("rep")
    row_count, width = rows.shape
    per_row = mass.shape[2] // capacity
    steps = [(a, b) for a in range(n_shard) for b in range(n_grp)]
    steps.sort(key=lambda s: -(ring_distance(s[0], n_shard) + ring_distance(s[1], n_grp)))
    away = steps[:-1]
    home = len(away)

    def chip(step):
        return lax.rem(shard + step[0], n_shard), lax.rem(grp + step[1], n_grp)

    def owner_of(step):
        z, x = chip(step)
        return z * n_grp + x

    def device(step, core):
        z, x = chip(step)
        return {"shard": z, "grp": x, "rep": core}

    my_owner = shard * n_grp + grp
    me = my_owner * n_rep + rep

    load = pltpu.make_async_copy(rows_hbm, rows, load_sem)
    load.start()
    barrier = pltpu.get_barrier_semaphore()

    def greet(step, core):
        pl.semaphore_signal(barrier, inc=1, device_id=device(step, core))

    for step in away:
        greet(step, 0)

    @pl.when(rep == 0)
    def _():
        for core in range(1, n_rep):
            for step in steps:
                greet(step, core)

    @pl.when(rep != 0)
    def _():
        greet((0, 0), 0)

    square = (row_count, row_count)
    down = lax.broadcasted_iota(jnp.int32, square, 0)
    across = lax.broadcasted_iota(jnp.int32, square, 1)
    cluster_row = cluster_ref[...]
    cluster_col = jnp.sum(
        jnp.where(down == across, jnp.broadcast_to(cluster_row, square), 0).astype(jnp.float32),
        axis=1, keepdims=True,
    ).astype(jnp.int32)
    same = cluster_col == cluster_row
    place_row = jnp.sum(jnp.where(same & (down < across), 1.0, 0.0), axis=0, keepdims=True).astype(jnp.int32)
    place_col = jnp.sum(jnp.where(same & (across < down), 1.0, 0.0), axis=1, keepdims=True).astype(jnp.int32)
    slot_row = cluster_row * capacity + place_row

    load.wait()
    matrix = rows[...]
    inverse = lax.rsqrt(jnp.sum(matrix * matrix, axis=1, keepdims=True) + 1e-06)
    unit = (matrix * inverse).astype(jnp.bfloat16)

    slot = lax.broadcasted_iota(jnp.int32, (capacity, row_count), 0)
    lead = lax.broadcasted_iota(jnp.int32, (capacity, width), 1) == 0

    def packed(step):
        chosen = jnp.where(slot + owner_of(step) * capacity == slot_row, 1.0, 0.0)
        block = jnp.dot(chosen.astype(jnp.bfloat16), unit, preferred_element_type=jnp.float32)
        vacant = jnp.sum(chosen, axis=1, keepdims=True) == 0.0
        return jnp.where(lead & vacant, 2.0, block).astype(jnp.bfloat16)

    for k, step in enumerate(away):
        outgoing[k] = packed(step)
    own = packed((0, 0))
    outgoing[home] = own

    @pl.when(rep == 0)
    def _():
        gathered[me] = own
        pl.semaphore_wait(barrier, n_shard * n_grp * n_rep - 1)

    @pl.when(rep != 0)
    def _():
        pl.semaphore_wait(barrier, n_shard * n_grp)

    def block_copy(k, step, source):
        return pltpu.make_async_remote_copy(
            src_ref=outgoing.at[k], dst_ref=gathered.at[source],
            send_sem=send_sem.at[k], recv_sem=recv_sem.at[source],
            device_id=device(step, 0),
        )

    for k, step in enumerate(away):
        block_copy(k, step, me).start()

    @pl.when(rep != 0)
    def _():
        block_copy(home, (0, 0), me).start()

    def reply(k, core):
        step = steps[k]
        target = owner_of(step) * n_rep + core
        return pltpu.make_async_remote_copy(
            src_ref=mass.at[target // per_row], dst_ref=returned.at[my_owner],
            send_sem=reply_send_sem.at[k * n_rep + core], recv_sem=reply_recv_sem.at[my_owner],
            device_id=device(step, core),
        )

    pairs = [(k, core) for k in range(len(steps)) for core in range(n_rep) if (k, core) != (home, 0)]

    @pl.when(rep == 0)
    def _():
        for k, core in reversed(pairs):
            block_copy(k, steps[k], owner_of(steps[k]) * n_rep + core).wait_recv()
        total = gathered.shape[0] * capacity
        members = gathered[...].reshape(total, width)
        live = members[:, 0:1].astype(jnp.float32) < 1.5
        lanes = mass.shape[2]
        group = 2 if mass.shape[0] % 2 == 0 else 1
        for first in range(0, mass.shape[0], group):
            span = group * lanes
            begin = first * lanes
            scores = lax.dot_general(
                members, members[begin : begin + span], (((1,), (1,)), ((), ())),
                preferred_element_type=jnp.float32,
            )
            query = lax.broadcasted_iota(jnp.int32, (total, span), 0)
            key = lax.broadcasted_iota(jnp.int32, (total, span), 1) + begin
            terms = jnp.where(live & (query != key), jnp.exp(sharpness * scores), 0.0)
            sums = jnp.sum(terms, axis=0, keepdims=True)
            for i in range(group):
                mass[first + i] = sums[:, i * lanes : (i + 1) * lanes]
        for k, core in pairs:
            reply(k, core).start()
        returned[my_owner] = mass[me // per_row]

    def reply_from(step):
        return pltpu.make_async_remote_copy(
            src_ref=mass.at[0], dst_ref=returned.at[owner_of(step)],
            send_sem=reply_send_sem.at[0], recv_sem=reply_recv_sem.at[owner_of(step)],
            device_id=device(step, 0),
        )

    for step in reversed(away):
        reply_from(step).wait_recv()

    @pl.when(rep != 0)
    def _():
        reply_from((0, 0)).wait_recv()

    lane = lax.broadcasted_iota(jnp.int32, (row_count, mass.shape[2]), 1)
    picked = jnp.zeros(lane.shape, jnp.float32)
    for owner in range(len(steps)):
        picked = jnp.where(cluster_col == owner, returned[owner], picked)
    mine = lane == lax.rem(me, per_row) * capacity + place_col
    column = jnp.sum(jnp.where(mine, picked, 0.0), axis=1, keepdims=True)
    mass_ref[...] = jnp.sum(jnp.where(down == across, column, 0.0), axis=0, keepdims=True)

    for k, step in enumerate(away):
        block_copy(k, step, me).wait_send()

    @pl.when(rep != 0)
    def _():
        block_copy(home, (0, 0), me).wait_send()

    @pl.when(rep == 0)
    def _():
        for k, core in pairs:
            reply(k, core).wait_send()


def kernel_body(sizes, embeddings, clusters):
    n_shard, n_grp, n_rep = sizes
    owners = n_shard * n_grp
    sources = owners * n_rep
    row_count, width = embeddings.shape
    capacity = 2 * row_count // owners
    lanes = 128
    mass = pl.pallas_call(
        functools.partial(kernel, sizes, capacity),
        out_shape=jax.ShapeDtypeStruct((1, row_count), jnp.float32),
        in_specs=[pl.BlockSpec(memory_space=pl.ANY), pl.BlockSpec(memory_space=pltpu.VMEM)],
        out_specs=pl.BlockSpec(memory_space=pltpu.VMEM),
        scratch_shapes=[
            pltpu.VMEM((row_count, width), jnp.float32),
            pltpu.VMEM((owners, capacity, width), jnp.bfloat16),
            pltpu.VMEM((sources, capacity, width), jnp.bfloat16),
            pltpu.VMEM((sources * capacity // lanes, 1, lanes), jnp.float32),
            pltpu.VMEM((owners, 1, lanes), jnp.float32),
            pltpu.SemaphoreType.DMA,
            pltpu.SemaphoreType.DMA((owners,)),
            pltpu.SemaphoreType.DMA((sources,)),
            pltpu.SemaphoreType.DMA((sources,)),
            pltpu.SemaphoreType.DMA((owners,)),
        ],
        compiler_params=pltpu.CompilerParams(collective_id=0, has_side_effects=True),
    )(embeddings, clusters.reshape(1, row_count))
    return jnp.log1p(mass.reshape(row_count))


def solution(mesh):
    sizes = (mesh.shape["shard"], mesh.shape["grp"], mesh.shape["rep"])
    placed = (P(("parts", "shard", "grp", "rep"), None), P(("parts", "shard", "grp", "rep"), None))

    def body(embeddings, clusters):
        row_count = embeddings.shape[0]
        capacity = 2 * row_count // (sizes[0] * sizes[1])
        if capacity % 16 == 0 and 128 % capacity == 0 and row_count % 128 == 0:
            return kernel_body(sizes, embeddings, clusters)
        return collective_body(embeddings, clusters)

    return jax.shard_map(
        body,
        mesh=mesh,
        in_specs=placed,
        out_specs=P(("parts", "shard", "grp", "rep")),
        check_vma=False,
    )
```

```python
import functools

import jax
import jax.numpy as jnp
from jax import lax
from jax.experimental import pallas as pl
from jax.experimental.pallas import tpu as pltpu
from jax.sharding import PartitionSpec as P

sharpness = 60.0


def from_partner(value, axis, distance):
    mask = 2**distance
    pairs = [(source, source ^ mask) for source in range(lax.axis_size(axis))]
    return lax.ppermute(value, axis, pairs)


def unit_rows(matrix):
    inverse = lax.rsqrt(jnp.sum(matrix * matrix, axis=1, keepdims=True) + 1e-06)
    return (matrix * inverse).astype(jnp.bfloat16)


def collective_body(embeddings, clusters):
    shard_count = lax.axis_size("shard")
    group_count = lax.axis_size("grp")
    owners = shard_count * group_count
    row_count = embeddings.shape[0]
    feature_dim = embeddings.shape[1]
    capacity = 2 * row_count // owners
    normed = unit_rows(embeddings)
    cluster_of = clusters[:, 0]
    member_table = (cluster_of[:, None] == jnp.arange(owners, dtype=jnp.int32)[None, :]).astype(
        jnp.float32
    )
    earlier = (jnp.arange(row_count)[:, None] > jnp.arange(row_count)[None, :]).astype(jnp.float32)
    preceding = jnp.dot(
        earlier, member_table, precision=lax.Precision.HIGHEST, preferred_element_type=jnp.float32
    )
    position = jnp.sum(preceding * member_table, axis=1).astype(jnp.int32)
    slot_index = cluster_of * capacity + position
    outgoing = jnp.zeros((owners * capacity, feature_dim), jnp.bfloat16).at[slot_index].set(normed)
    present = jnp.zeros((owners * capacity,), jnp.int32).at[slot_index].set(1)
    arrived, arrived_live = (
        lax.all_to_all(
            outgoing.reshape(owners, capacity, feature_dim),
            ("shard", "grp"),
            split_axis=0,
            concat_axis=0,
            tiled=True,
        ),
        lax.all_to_all(
            present.reshape(owners, capacity),
            ("shard", "grp"),
            split_axis=0,
            concat_axis=0,
            tiled=True,
        ),
    )
    slot_count = owners * capacity
    local_rows = arrived.reshape(slot_count, feature_dim)
    local_live = arrived_live.reshape(slot_count)
    partner, partner_live = from_partner((local_rows, local_live), "rep", 0)
    key_rows = jnp.concatenate([local_rows, partner], axis=0)
    key_live = jnp.concatenate([local_live, partner_live], axis=0) > 0
    key_pos = jnp.arange(2 * slot_count, dtype=jnp.int32)

    def block_sums(block_index):
        first_row = block_index * slot_count
        scores = lax.dot_general(
            local_rows, key_rows, (((1,), (1,)), ((), ())), preferred_element_type=jnp.float32
        )
        query_pos = first_row + jnp.arange(slot_count, dtype=jnp.int32)
        paired = key_live[None, :] & (query_pos[:, None] != key_pos[None, :])
        return jnp.sum(jnp.where(paired, jnp.exp(sharpness * scores), 0.0), axis=1)

    partial_mass = lax.map(
        block_sums, jnp.arange(slot_count // slot_count, dtype=jnp.int32)
    ).reshape(slot_count)
    returned = lax.all_to_all(
        partial_mass.reshape(owners, capacity),
        ("shard", "grp"),
        split_axis=0,
        concat_axis=0,
        tiled=True,
    )
    mass = returned.reshape(slot_count)[slot_index]
    return jnp.log1p(mass)


def ring_distance(step, size):
    return min(step, size - step)


def kernel(sizes, capacity, rows_hbm, cluster_ref, mass_ref, rows, outgoing, gathered, mass, returned,
           load_sem, send_sem, recv_sem, reply_send_sem, reply_recv_sem, ahead_sem, behind_sem):
    n_shard, n_grp, n_rep = sizes
    shard, grp, rep = lax.axis_index("shard"), lax.axis_index("grp"), lax.axis_index("rep")
    row_count, width = rows.shape
    per_row = mass.shape[2] // capacity
    steps = [(a, b) for a in range(n_shard) for b in range(n_grp)]
    steps.sort(key=lambda s: -(ring_distance(s[0], n_shard) + ring_distance(s[1], n_grp)))
    away = steps[:-1]
    home = len(away)

    def chip(step):
        return lax.rem(shard + step[0], n_shard), lax.rem(grp + step[1], n_grp)

    def owner_of(step):
        z, x = chip(step)
        return z * n_grp + x

    def device(step, core):
        z, x = chip(step)
        return {"shard": z, "grp": x, "rep": core}

    my_owner = shard * n_grp + grp
    me = my_owner * n_rep + rep

    load = pltpu.make_async_copy(rows_hbm, rows, load_sem)
    load.start()
    barrier = pltpu.get_barrier_semaphore()

    def greet(step, core):
        pl.semaphore_signal(barrier, inc=1, device_id=device(step, core))

    has_next, has_last = shard + 1 < n_shard, shard > 0
    forward, backward = (1, 0), (n_shard - 1, 0)

    def greet_plane(a):
        for b in range(n_grp):
            if (a, b) != (0, 0):
                greet((a, b), 0)

        @pl.when(rep == 0)
        def _():
            for b in range(n_grp):
                for core in range(1, n_rep):
                    greet((a, b), core)

        if a:
            @pl.when(rep != 0)
            def _():
                greet((a, 0), rep)

    pl.when(has_next)(lambda: greet_plane(1))
    pl.when(has_last)(lambda: greet_plane(n_shard - 1))
    greet_plane(0)

    @pl.when(rep != 0)
    def _():
        greet((0, 0), 0)

    square = (row_count, row_count)
    down = lax.broadcasted_iota(jnp.int32, square, 0)
    across = lax.broadcasted_iota(jnp.int32, square, 1)
    cluster_row = cluster_ref[...]
    cluster_col = jnp.sum(
        jnp.where(down == across, jnp.broadcast_to(cluster_row, square), 0).astype(jnp.float32),
        axis=1, keepdims=True,
    ).astype(jnp.int32)
    same = cluster_col == cluster_row
    place_row = jnp.sum(jnp.where(same & (down < across), 1.0, 0.0), axis=0, keepdims=True).astype(jnp.int32)
    place_col = jnp.sum(jnp.where(same & (across < down), 1.0, 0.0), axis=1, keepdims=True).astype(jnp.int32)
    slot_row = cluster_row * capacity + place_row

    load.wait()
    matrix = rows[...]
    inverse = lax.rsqrt(jnp.sum(matrix * matrix, axis=1, keepdims=True) + 1e-06)
    unit = (matrix * inverse).astype(jnp.bfloat16)

    slot = lax.broadcasted_iota(jnp.int32, (capacity, row_count), 0)
    lead = lax.broadcasted_iota(jnp.int32, (capacity, width), 1) == 0

    def packed(step):
        chosen = jnp.where(slot + owner_of(step) * capacity == slot_row, 1.0, 0.0)
        block = jnp.dot(chosen.astype(jnp.bfloat16), unit, preferred_element_type=jnp.float32)
        vacant = jnp.sum(chosen, axis=1, keepdims=True) == 0.0
        return jnp.where(lead & vacant, 2.0, block).astype(jnp.bfloat16)

    for k, step in enumerate(away):
        outgoing[k] = packed(step)
    own = packed((0, 0))
    outgoing[home] = own
    beside = jnp.where(has_next, 1, 0) + jnp.where(has_last, 1, 0)

    @pl.when(rep == 0)
    def _():
        gathered[me] = own
        pl.semaphore_wait(barrier, beside * n_grp * n_rep + n_grp * n_rep - 1)

    @pl.when(rep != 0)
    def _():
        pl.semaphore_wait(barrier, beside * (n_grp + 1) + n_grp)

    def block_copy(k, step, source):
        return pltpu.make_async_remote_copy(
            src_ref=outgoing.at[k], dst_ref=gathered.at[source],
            send_sem=send_sem.at[k], recv_sem=recv_sem.at[source],
            device_id=device(step, 0),
        )

    def send(a, b):
        block_copy(steps.index((a, b)), (a, b), me).start()

    def tell(sem, distance, step):
        pl.semaphore_signal(sem.at[distance], inc=1, device_id=device(step, rep))

    @pl.when(has_next & has_last)
    def _():
        if n_shard > 2:
            tell(ahead_sem, 2, backward)
            tell(behind_sem, 2, forward)

    def send_beside(b):
        pl.when(has_next)(lambda: send(1, b))
        if n_shard > 2:
            pl.when(has_last)(lambda: send(n_shard - 1, b))

    send_beside(n_grp - 1)
    for distance in range(2, n_shard):
        @pl.when(shard + distance < n_shard)
        def _():
            pl.semaphore_wait(ahead_sem.at[distance], 1)
            if distance + 1 < n_shard:
                pl.when(has_last)(lambda: tell(ahead_sem, distance + 1, backward))

        @pl.when(shard >= distance)
        def _():
            pl.semaphore_wait(behind_sem.at[distance], 1)
            if distance + 1 < n_shard:
                pl.when(has_next)(lambda: tell(behind_sem, distance + 1, forward))

    for distance in reversed(range(2, n_shard)):
        for b in reversed(range(n_grp)):
            pl.when(shard + distance < n_shard)(lambda: send(distance, b))
            pl.when(shard >= distance)(lambda: send(n_shard - distance, b))
    for b in reversed(range(n_grp - 1)):
        send_beside(b)
    for b in range(1, n_grp):
        send(0, b)

    @pl.when(rep != 0)
    def _():
        block_copy(home, (0, 0), me).start()

    def reply(k, core):
        step = steps[k]
        target = owner_of(step) * n_rep + core
        return pltpu.make_async_remote_copy(
            src_ref=mass.at[target // per_row], dst_ref=returned.at[my_owner],
            send_sem=reply_send_sem.at[k * n_rep + core], recv_sem=reply_recv_sem.at[my_owner],
            device_id=device(step, core),
        )

    pairs = [(k, core) for k in range(len(steps)) for core in range(n_rep) if (k, core) != (home, 0)]

    @pl.when(rep == 0)
    def _():
        for k, core in reversed(pairs):
            block_copy(k, steps[k], owner_of(steps[k]) * n_rep + core).wait_recv()
        total = gathered.shape[0] * capacity
        members = gathered[...].reshape(total, width)
        live = members[:, 0:1].astype(jnp.float32) < 1.5
        lanes = mass.shape[2]
        group = 2 if mass.shape[0] % 2 == 0 else 1
        for first in range(0, mass.shape[0], group):
            span = group * lanes
            begin = first * lanes
            scores = lax.dot_general(
                members, members[begin : begin + span], (((1,), (1,)), ((), ())),
                preferred_element_type=jnp.float32,
            )
            query = lax.broadcasted_iota(jnp.int32, (total, span), 0)
            key = lax.broadcasted_iota(jnp.int32, (total, span), 1) + begin
            terms = jnp.where(live & (query != key), jnp.exp(sharpness * scores), 0.0)
            sums = jnp.sum(terms, axis=0, keepdims=True)
            for i in range(group):
                mass[first + i] = sums[:, i * lanes : (i + 1) * lanes]
        for k, core in pairs:
            reply(k, core).start()
        returned[my_owner] = mass[me // per_row]

    def reply_from(step):
        return pltpu.make_async_remote_copy(
            src_ref=mass.at[0], dst_ref=returned.at[owner_of(step)],
            send_sem=reply_send_sem.at[0], recv_sem=reply_recv_sem.at[owner_of(step)],
            device_id=device(step, 0),
        )

    for step in reversed(away):
        reply_from(step).wait_recv()

    @pl.when(rep != 0)
    def _():
        reply_from((0, 0)).wait_recv()

    lane = lax.broadcasted_iota(jnp.int32, (row_count, mass.shape[2]), 1)
    picked = jnp.zeros(lane.shape, jnp.float32)
    for owner in range(len(steps)):
        picked = jnp.where(cluster_col == owner, returned[owner], picked)
    mine = lane == lax.rem(me, per_row) * capacity + place_col
    column = jnp.sum(jnp.where(mine, picked, 0.0), axis=1, keepdims=True)
    mass_ref[...] = jnp.sum(jnp.where(down == across, column, 0.0), axis=0, keepdims=True)

    for k, step in enumerate(away):
        block_copy(k, step, me).wait_send()

    @pl.when(rep != 0)
    def _():
        block_copy(home, (0, 0), me).wait_send()

    @pl.when(rep == 0)
    def _():
        for k, core in pairs:
            reply(k, core).wait_send()


def kernel_body(sizes, embeddings, clusters):
    n_shard, n_grp, n_rep = sizes
    owners = n_shard * n_grp
    sources = owners * n_rep
    row_count, width = embeddings.shape
    capacity = 2 * row_count // owners
    lanes = 128
    mass = pl.pallas_call(
        functools.partial(kernel, sizes, capacity),
        out_shape=jax.ShapeDtypeStruct((1, row_count), jnp.float32),
        in_specs=[pl.BlockSpec(memory_space=pl.ANY), pl.BlockSpec(memory_space=pltpu.VMEM)],
        out_specs=pl.BlockSpec(memory_space=pltpu.VMEM),
        scratch_shapes=[
            pltpu.VMEM((row_count, width), jnp.float32),
            pltpu.VMEM((owners, capacity, width), jnp.bfloat16),
            pltpu.VMEM((sources, capacity, width), jnp.bfloat16),
            pltpu.VMEM((sources * capacity // lanes, 1, lanes), jnp.float32),
            pltpu.VMEM((owners, 1, lanes), jnp.float32),
            pltpu.SemaphoreType.DMA,
            pltpu.SemaphoreType.DMA((owners,)),
            pltpu.SemaphoreType.DMA((sources,)),
            pltpu.SemaphoreType.DMA((sources,)),
            pltpu.SemaphoreType.DMA((owners,)),
            pltpu.SemaphoreType.REGULAR((n_shard,)),
            pltpu.SemaphoreType.REGULAR((n_shard,)),
        ],
        compiler_params=pltpu.CompilerParams(collective_id=0, has_side_effects=True),
    )(embeddings, clusters.reshape(1, row_count))
    return jnp.log1p(mass.reshape(row_count))


def solution(mesh):
    sizes = (mesh.shape["shard"], mesh.shape["grp"], mesh.shape["rep"])
    placed = (P(("parts", "shard", "grp", "rep"), None), P(("parts", "shard", "grp", "rep"), None))

    def body(embeddings, clusters):
        row_count = embeddings.shape[0]
        capacity = 2 * row_count // (sizes[0] * sizes[1])
        if capacity % 16 == 0 and 128 % capacity == 0 and row_count % 128 == 0:
            return kernel_body(sizes, embeddings, clusters)
        return collective_body(embeddings, clusters)

    return jax.shard_map(
        body,
        mesh=mesh,
        in_specs=placed,
        out_specs=P(("parts", "shard", "grp", "rep")),
        check_vma=False,
    )
```

```python
import functools

import jax
import jax.numpy as jnp
from jax import lax
from jax.experimental import pallas as pl
from jax.experimental.pallas import tpu as pltpu
from jax.sharding import PartitionSpec as P

sharpness = 60.0


def from_partner(value, axis, distance):
    mask = 2**distance
    pairs = [(source, source ^ mask) for source in range(lax.axis_size(axis))]
    return lax.ppermute(value, axis, pairs)


def unit_rows(matrix):
    inverse = lax.rsqrt(jnp.sum(matrix * matrix, axis=1, keepdims=True) + 1e-06)
    return (matrix * inverse).astype(jnp.bfloat16)


def collective_body(embeddings, clusters):
    shard_count = lax.axis_size("shard")
    group_count = lax.axis_size("grp")
    owners = shard_count * group_count
    row_count = embeddings.shape[0]
    feature_dim = embeddings.shape[1]
    capacity = 2 * row_count // owners
    normed = unit_rows(embeddings)
    cluster_of = clusters[:, 0]
    member_table = (cluster_of[:, None] == jnp.arange(owners, dtype=jnp.int32)[None, :]).astype(
        jnp.float32
    )
    earlier = (jnp.arange(row_count)[:, None] > jnp.arange(row_count)[None, :]).astype(jnp.float32)
    preceding = jnp.dot(
        earlier, member_table, precision=lax.Precision.HIGHEST, preferred_element_type=jnp.float32
    )
    position = jnp.sum(preceding * member_table, axis=1).astype(jnp.int32)
    slot_index = cluster_of * capacity + position
    outgoing = jnp.zeros((owners * capacity, feature_dim), jnp.bfloat16).at[slot_index].set(normed)
    present = jnp.zeros((owners * capacity,), jnp.int32).at[slot_index].set(1)
    arrived, arrived_live = (
        lax.all_to_all(
            outgoing.reshape(owners, capacity, feature_dim),
            ("shard", "grp"),
            split_axis=0,
            concat_axis=0,
            tiled=True,
        ),
        lax.all_to_all(
            present.reshape(owners, capacity),
            ("shard", "grp"),
            split_axis=0,
            concat_axis=0,
            tiled=True,
        ),
    )
    slot_count = owners * capacity
    local_rows = arrived.reshape(slot_count, feature_dim)
    local_live = arrived_live.reshape(slot_count)
    partner, partner_live = from_partner((local_rows, local_live), "rep", 0)
    key_rows = jnp.concatenate([local_rows, partner], axis=0)
    key_live = jnp.concatenate([local_live, partner_live], axis=0) > 0
    key_pos = jnp.arange(2 * slot_count, dtype=jnp.int32)

    def block_sums(block_index):
        first_row = block_index * slot_count
        scores = lax.dot_general(
            local_rows, key_rows, (((1,), (1,)), ((), ())), preferred_element_type=jnp.float32
        )
        query_pos = first_row + jnp.arange(slot_count, dtype=jnp.int32)
        paired = key_live[None, :] & (query_pos[:, None] != key_pos[None, :])
        return jnp.sum(jnp.where(paired, jnp.exp(sharpness * scores), 0.0), axis=1)

    partial_mass = lax.map(
        block_sums, jnp.arange(slot_count // slot_count, dtype=jnp.int32)
    ).reshape(slot_count)
    returned = lax.all_to_all(
        partial_mass.reshape(owners, capacity),
        ("shard", "grp"),
        split_axis=0,
        concat_axis=0,
        tiled=True,
    )
    mass = returned.reshape(slot_count)[slot_index]
    return jnp.log1p(mass)


def ring_distance(step, size):
    return min(step, size - step)


def kernel(sizes, capacity, rows_hbm, cluster_ref, mass_ref, rows, outgoing, gathered, mass, returned,
           load_sem, send_sem, recv_sem, reply_send_sem, reply_recv_sem, ahead_sem, behind_sem):
    n_shard, n_grp, n_rep = sizes
    shard, grp, rep = lax.axis_index("shard"), lax.axis_index("grp"), lax.axis_index("rep")
    row_count, width = rows.shape
    per_row = mass.shape[2] // capacity
    steps = [(a, b) for a in range(n_shard) for b in range(n_grp)]
    steps.sort(key=lambda s: -(ring_distance(s[0], n_shard) + ring_distance(s[1], n_grp)))
    away = steps[:-1]
    home = len(away)

    def chip(step):
        return lax.rem(shard + step[0], n_shard), lax.rem(grp + step[1], n_grp)

    def owner_of(step):
        z, x = chip(step)
        return z * n_grp + x

    def device(step, core):
        z, x = chip(step)
        return {"shard": z, "grp": x, "rep": core}

    my_owner = shard * n_grp + grp
    me = my_owner * n_rep + rep

    load = pltpu.make_async_copy(rows_hbm, rows, load_sem)
    load.start()
    barrier = pltpu.get_barrier_semaphore()

    def greet(step, core):
        pl.semaphore_signal(barrier, inc=1, device_id=device(step, core))

    has_next, has_last = shard + 1 < n_shard, shard > 0
    forward, backward = (1, 0), (n_shard - 1, 0)

    def greet_plane(a):
        for b in range(n_grp):
            if (a, b) != (0, 0):
                greet((a, b), 0)

        @pl.when(rep == 0)
        def _():
            for b in range(n_grp):
                for core in range(1, n_rep):
                    greet((a, b), core)

        if a:
            @pl.when(rep != 0)
            def _():
                greet((a, 0), rep)

    pl.when(has_next)(lambda: greet_plane(1))
    pl.when(has_last)(lambda: greet_plane(n_shard - 1))
    greet_plane(0)

    @pl.when(rep != 0)
    def _():
        greet((0, 0), 0)

    square = (row_count, row_count)
    down = lax.broadcasted_iota(jnp.int32, square, 0)
    across = lax.broadcasted_iota(jnp.int32, square, 1)
    cluster_row = cluster_ref[...]
    cluster_col = jnp.sum(
        jnp.where(down == across, jnp.broadcast_to(cluster_row, square), 0).astype(jnp.float32),
        axis=1, keepdims=True,
    ).astype(jnp.int32)
    same = cluster_col == cluster_row
    place_row = jnp.sum(jnp.where(same & (down < across), 1.0, 0.0), axis=0, keepdims=True).astype(jnp.int32)
    place_col = jnp.sum(jnp.where(same & (across < down), 1.0, 0.0), axis=1, keepdims=True).astype(jnp.int32)
    slot_row = cluster_row * capacity + place_row

    load.wait()
    matrix = rows[...]
    inverse = lax.rsqrt(jnp.sum(matrix * matrix, axis=1, keepdims=True) + 1e-06)
    unit = (matrix * inverse).astype(jnp.bfloat16)

    slot = lax.broadcasted_iota(jnp.int32, (capacity, row_count), 0)
    lead = lax.broadcasted_iota(jnp.int32, (capacity, width), 1) == 0

    def packed(step):
        chosen = jnp.where(slot + owner_of(step) * capacity == slot_row, 1.0, 0.0)
        block = jnp.dot(chosen.astype(jnp.bfloat16), unit, preferred_element_type=jnp.float32)
        vacant = jnp.sum(chosen, axis=1, keepdims=True) == 0.0
        return jnp.where(lead & vacant, 2.0, block).astype(jnp.bfloat16)

    for k, step in enumerate(away):
        outgoing[k] = packed(step)
    own = packed((0, 0))
    outgoing[home] = own
    beside = jnp.where(has_next, 1, 0) + jnp.where(has_last, 1, 0)

    @pl.when(rep == 0)
    def _():
        gathered[me] = own
        pl.semaphore_wait(barrier, beside * n_grp * n_rep + n_grp * n_rep - 1)

    @pl.when(rep != 0)
    def _():
        pl.semaphore_wait(barrier, beside * (n_grp + 1) + n_grp)

    def block_copy(k, step, source):
        return pltpu.make_async_remote_copy(
            src_ref=outgoing.at[k], dst_ref=gathered.at[source],
            send_sem=send_sem.at[k], recv_sem=recv_sem.at[source],
            device_id=device(step, 0),
        )

    def send(a, b):
        block_copy(steps.index((a, b)), (a, b), me).start()

    def tell(sem, distance, step):
        pl.semaphore_signal(sem.at[distance], inc=1, device_id=device(step, rep))

    @pl.when(has_next & has_last)
    def _():
        if n_shard > 2:
            tell(ahead_sem, 2, backward)
            tell(behind_sem, 2, forward)

    def send_beside(b):
        pl.when(has_next)(lambda: send(1, b))
        if n_shard > 2:
            pl.when(has_last)(lambda: send(n_shard - 1, b))

    send_beside(n_grp - 1)
    for distance in range(2, n_shard):
        @pl.when(shard + distance < n_shard)
        def _():
            pl.semaphore_wait(ahead_sem.at[distance], 1)
            if distance + 1 < n_shard:
                pl.when(has_last)(lambda: tell(ahead_sem, distance + 1, backward))

        @pl.when(shard >= distance)
        def _():
            pl.semaphore_wait(behind_sem.at[distance], 1)
            if distance + 1 < n_shard:
                pl.when(has_next)(lambda: tell(behind_sem, distance + 1, forward))

    for distance in reversed(range(2, n_shard)):
        for b in reversed(range(n_grp)):
            pl.when(shard + distance < n_shard)(lambda: send(distance, b))
            pl.when(shard >= distance)(lambda: send(n_shard - distance, b))
    for b in reversed(range(n_grp - 1)):
        send_beside(b)
    for b in range(1, n_grp):
        send(0, b)

    @pl.when(rep != 0)
    def _():
        block_copy(home, (0, 0), me).start()

    def reply(k, core):
        step = steps[k]
        target = owner_of(step) * n_rep + core
        return pltpu.make_async_remote_copy(
            src_ref=mass.at[target // per_row], dst_ref=returned.at[my_owner],
            send_sem=reply_send_sem.at[k * n_rep + core], recv_sem=reply_recv_sem.at[my_owner],
            device_id=device(step, core),
        )

    pairs = [(k, core) for k in range(len(steps)) for core in range(n_rep) if (k, core) != (home, 0)]

    @pl.when(rep == 0)
    def _():
        half = gathered.shape[0] // 2
        near = jnp.where(2 * shard >= n_shard, half, 0)
        far = half - near
        span = half * capacity

        def arrivals(wanted):
            for k, core in reversed(pairs):
                source = owner_of(steps[k]) * n_rep + core
                here = (source >= near) & (source < near + half)
                pl.when(here if wanted else jnp.logical_not(here))(block_copy(k, steps[k], source).wait_recv)

        def sums(queries, keys, same_half):
            scores = lax.dot_general(
                queries, keys, (((1,), (1,)), ((), ())), preferred_element_type=jnp.float32
            )
            counted = queries[:, 0:1].astype(jnp.float32) < 1.5
            if same_half:
                counted = counted & (
                    lax.broadcasted_iota(jnp.int32, scores.shape, 0)
                    != lax.broadcasted_iota(jnp.int32, scores.shape, 1)
                )
            return jnp.sum(jnp.where(counted, jnp.exp(sharpness * scores), 0.0), axis=0, keepdims=True)

        arrivals(True)
        mine = gathered[pl.ds(near, half)].reshape(span, width)
        partial = sums(mine, mine, True)
        arrivals(False)
        theirs = gathered[pl.ds(far, half)].reshape(span, width)
        lanes = mass.shape[2]
        for first, total in (
            (near, partial + sums(theirs, mine, False)),
            (far, sums(mine, theirs, False) + sums(theirs, theirs, True)),
        ):
            for i in range(span // lanes):
                mass[first // per_row + i] = total[:, i * lanes : (i + 1) * lanes]
        for k, core in pairs:
            reply(k, core).start()
        returned[my_owner] = mass[me // per_row]

    def reply_from(step):
        return pltpu.make_async_remote_copy(
            src_ref=mass.at[0], dst_ref=returned.at[owner_of(step)],
            send_sem=reply_send_sem.at[0], recv_sem=reply_recv_sem.at[owner_of(step)],
            device_id=device(step, 0),
        )

    for step in reversed(away):
        reply_from(step).wait_recv()

    @pl.when(rep != 0)
    def _():
        reply_from((0, 0)).wait_recv()

    lane = lax.broadcasted_iota(jnp.int32, (row_count, mass.shape[2]), 1)
    picked = jnp.zeros(lane.shape, jnp.float32)
    for owner in range(len(steps)):
        picked = jnp.where(cluster_col == owner, returned[owner], picked)
    mine = lane == lax.rem(me, per_row) * capacity + place_col
    column = jnp.sum(jnp.where(mine, picked, 0.0), axis=1, keepdims=True)
    mass_ref[...] = jnp.sum(jnp.where(down == across, column, 0.0), axis=0, keepdims=True)

    for k, step in enumerate(away):
        block_copy(k, step, me).wait_send()

    @pl.when(rep != 0)
    def _():
        block_copy(home, (0, 0), me).wait_send()

    @pl.when(rep == 0)
    def _():
        for k, core in pairs:
            reply(k, core).wait_send()


def kernel_body(sizes, embeddings, clusters):
    n_shard, n_grp, n_rep = sizes
    owners = n_shard * n_grp
    sources = owners * n_rep
    row_count, width = embeddings.shape
    capacity = 2 * row_count // owners
    lanes = 128
    mass = pl.pallas_call(
        functools.partial(kernel, sizes, capacity),
        out_shape=jax.ShapeDtypeStruct((1, row_count), jnp.float32),
        in_specs=[pl.BlockSpec(memory_space=pl.ANY), pl.BlockSpec(memory_space=pltpu.VMEM)],
        out_specs=pl.BlockSpec(memory_space=pltpu.VMEM),
        scratch_shapes=[
            pltpu.VMEM((row_count, width), jnp.float32),
            pltpu.VMEM((owners, capacity, width), jnp.bfloat16),
            pltpu.VMEM((sources, capacity, width), jnp.bfloat16),
            pltpu.VMEM((sources * capacity // lanes, 1, lanes), jnp.float32),
            pltpu.VMEM((owners, 1, lanes), jnp.float32),
            pltpu.SemaphoreType.DMA,
            pltpu.SemaphoreType.DMA((owners,)),
            pltpu.SemaphoreType.DMA((sources,)),
            pltpu.SemaphoreType.DMA((sources,)),
            pltpu.SemaphoreType.DMA((owners,)),
            pltpu.SemaphoreType.REGULAR((n_shard,)),
            pltpu.SemaphoreType.REGULAR((n_shard,)),
        ],
        compiler_params=pltpu.CompilerParams(collective_id=0, has_side_effects=True),
    )(embeddings, clusters.reshape(1, row_count))
    return jnp.log1p(mass.reshape(row_count))


def solution(mesh):
    sizes = (mesh.shape["shard"], mesh.shape["grp"], mesh.shape["rep"])
    placed = (P(("parts", "shard", "grp", "rep"), None), P(("parts", "shard", "grp", "rep"), None))

    def body(embeddings, clusters):
        row_count = embeddings.shape[0]
        owners = sizes[0] * sizes[1]
        capacity = 2 * row_count // owners
        if capacity % 16 == 0 and 128 % capacity == 0 and row_count % 128 == 0 and owners * capacity % 128 == 0:
            return kernel_body(sizes, embeddings, clusters)
        return collective_body(embeddings, clusters)

    return jax.shard_map(
        body,
        mesh=mesh,
        in_specs=placed,
        out_specs=P(("parts", "shard", "grp", "rep")),
        check_vma=False,
    )
```
